32 devices in a mesh: grid: 8 (over z, y), vec: 4 (over x, core).
Axes of the slice: x: 2, y: 2, z: 4, core: 2. Of those that a mesh axis runs over, the one named last changes fastest.
Arguments:
- trial_block: float32 [16, 48, 32, 128], P('vec', 'grid'), may hold values from -60 to 60, as said below
- response_weight: float32 [48, 32, 128], P('grid'), may hold values from 2 to 5
Outputs:
- rotated: float32 [16, 48, 32, 128], P('vec', 'grid')
- potentials: float32 [16, 48, 32, 128], P('vec', 'grid')
- ritz_matrix: float32 [16, 16], replicated
The draws below stay inside these ranges and needn't reach their ends.
Inputs may be any that keep to these rules, and one draw needn't show every extreme that they name: `trial_block`: trial vectors whose Gram matrix is positive definite.
All inputs are finite; a program needn't handle non-finite values.
Results may differ from the reference program's by a relative error of at most 0.0002.
Values sent between devices are 32-bit elements; how exact they have to be, the bound alone decides.
A program may use at most 64 MiB of HBM per device.

```python
import math
import jax
import jax.numpy as jnp
from jax import lax

NVEC = 16
ITERS = 3
BX = 6
BY = 32
NZ = 128
GY = 2
GX = 4
NX = 24
NY = 64
ROWS = 48


def draw_trial_block(key, part):
    key_list = jax.random.split(jax.random.fold_in(key, 11), 9)
    shape = (NVEC, NX, NY, NZ)
    base_noise = jnp.clip(jax.random.normal(key_list[0], shape, jnp.float32), -6.0, 6.0)
    mix_weight = 0.3
    mixing = jnp.eye(NVEC, dtype=jnp.float32) + mix_weight * jax.random.normal(key_list[1], (NVEC, NVEC), jnp.float32) / jnp.sqrt(NVEC * 1.0)
    rough = jnp.tensordot(mixing, base_noise, axes=(1, 0), precision=lax.Precision.HIGHEST)
    coord_x = (jnp.arange(NX, dtype=jnp.float32) + 0.5) / NX
    coord_y = (jnp.arange(NY, dtype=jnp.float32) + 0.5) / NY
    coord_z = (jnp.arange(NZ, dtype=jnp.float32) + 0.5) / NZ
    tilt_share = jax.random.uniform(key_list[2], (NVEC,), jnp.float32, 0.2, 0.8)
    flip_side = jax.random.randint(key_list[3], (NVEC,), 0, 2).astype(jnp.float32)
    slope = tilt_share[:, None, None] * coord_x[None, :, None] + (1.0 - tilt_share)[:, None, None] * coord_y[None, None, :]
    slope = flip_side[:, None, None] * (1.0 - slope) + (1.0 - flip_side[:, None, None]) * slope
    envelope = jnp.exp(2.3025851 * (slope - 1.0))
    waves = jax.random.randint(key_list[4], (3, NVEC, 3), 1, 4).astype(jnp.float32)
    phases = jax.random.uniform(key_list[5], (3, NVEC), jnp.float32, 0.0, 6.2831853)
    smooth_gain = jnp.exp(jax.random.uniform(key_list[6], (NVEC,), jnp.float32, -1.2039728, 0.9162907))
    smooth = jnp.zeros(shape, jnp.float32)
    for mode_index in range(3):
        wave_x = waves[mode_index, :, 0][:, None, None, None] * coord_x[None, :, None, None]
        wave_y = waves[mode_index, :, 1][:, None, None, None] * coord_y[None, None, :, None]
        wave_z = waves[mode_index, :, 2][:, None, None, None] * coord_z[None, None, None, :]
        wave_angle = 6.2831853 * (wave_x + wave_y + wave_z) + phases[mode_index][:, None, None, None]
        smooth = smooth + 0.8 * jnp.cos(wave_angle)
    scales = jnp.exp(jax.random.uniform(key_list[8], (NVEC,), jnp.float32, 0.0, 1.3862944))
    total = envelope[:, :, :, None] * rough + smooth_gain[:, None, None, None] * smooth
    result = jnp.clip(scales[:, None, None, None] * total, -60.0, 60.0)
    blocks = result.reshape(NVEC, GX, BX, GY, BY, NZ)
    stored = jnp.swapaxes(blocks, 2, 3).reshape(NVEC, GX * GY * BX, BY, NZ)
    return stored.astype(jnp.float32)


def block_scale(key, dims, cuts, least, largest):
    factor_of, own = 1.0, jax.random.fold_in(key, 6)
    for dim, shards_of in cuts:
        draws = jnp.exp(jax.random.uniform(jax.random.fold_in(own, dim), (shards_of,), jnp.float32, least / len(cuts), largest / len(cuts)))
        factor_of = factor_of * jnp.repeat(draws, dims[dim] // shards_of).reshape([-1 if axis == dim else 1 for axis in range(len(dims))])
    return factor_of


def setup_inputs(seed: int = 0) -> dict:
    arg_keys = jax.random.split(jax.random.key(seed), 3)
    trial_block = draw_trial_block(jax.random.fold_in(arg_keys[2], 71), 0)
    response_weight = jnp.clip(jnp.exp(math.log(5.0) - 0.916290732 * jax.random.uniform(arg_keys[1], (ROWS, BY, NZ), jnp.float32) ** block_scale(arg_keys[1], (ROWS, BY, NZ), ((0, 8),), -0.2, 0.2)), 2.0, 5.0)
    return {"trial_block": trial_block, "response_weight": response_weight}


COEFFS = (-5369.0 / 1800.0, 12.0 / 7.0, -15.0 / 56.0, 10.0 / 189.0, -1.0 / 112.0, 2.0 / 1925.0, -1.0 / 16632.0)

def to_grid(field):
    leading = field.shape[:-3]
    blocks = field.reshape(leading + (GX, GY, BX, BY, NZ))
    return jnp.swapaxes(blocks, -4, -3).reshape(leading + (NX, NY, NZ))

def to_store(field):
    leading = field.shape[:-3]
    blocks = field.reshape(leading + (GX, BX, GY, BY, NZ))
    return jnp.swapaxes(blocks, -4, -3).reshape(leading + (GX * GY * BX, BY, NZ))

def along_axis(total, padded, axis, length):
    for offset in range(1, 7):
        upper = lax.slice_in_dim(padded, 6 + offset, 6 + offset + length, axis=axis)
        lower = lax.slice_in_dim(padded, 6 - offset, 6 - offset + length, axis=axis)
        total = total + COEFFS[offset] * (upper + lower)
    return total

def operate(field):
    total = 3.0 * COEFFS[0] * field
    padded_x = jnp.concatenate([field[NX - 6:], field, field[:6]], axis=0)
    total = along_axis(total, padded_x, 0, NX)
    sheared_up = jnp.roll(field, -BX, axis=0)
    sheared_down = jnp.roll(field, BX, axis=0)
    padded_y = jnp.concatenate([sheared_down[:, NY - 6:], field, sheared_up[:, :6]], axis=1)
    total = along_axis(total, padded_y, 1, NY)
    padded_z = jnp.pad(field, ((0, 0), (0, 0), (6, 6)))
    total = along_axis(total, padded_z, 2, NZ)
    return -total

def solve_one(source):
    solution = jnp.zeros_like(source)
    residual = source
    direction = source
    norm_now = jnp.sum(residual * residual)
    for step in range(ITERS):
        image = operate(direction)
        alpha = norm_now / jnp.sum(direction * image)
        solution = solution + alpha * direction
        residual = residual - alpha * image
        norm_next = jnp.sum(residual * residual)
        direction = residual + norm_next / norm_now * direction
        norm_now = norm_next
    return solution

def reference(trial_block, response_weight):
    weight_grid = to_grid(response_weight)
    phi_grid = lax.map(lambda vector: solve_one(weight_grid * vector), to_grid(trial_block))
    phi = to_store(phi_grid)
    cells = NX * NY * NZ
    flat_x = trial_block.reshape(NVEC, -1)
    flat_p = phi.reshape(NVEC, -1)
    high = lax.Precision.HIGHEST
    gram = jnp.dot(flat_x, flat_x.T, precision=high) / cells
    cross = jnp.dot(flat_x, flat_p.T, precision=high) / cells
    lower = jnp.linalg.cholesky(gram)
    inverse = lax.linalg.triangular_solve(lower, jnp.eye(NVEC, dtype=jnp.float32), left_side=True, lower=True)
    middle = jnp.dot(inverse, 0.5 * (cross + cross.T), precision=high)
    ritz_matrix = jnp.dot(middle, inverse.T, precision=high)
    rotated = jnp.dot(inverse, flat_x, precision=high).reshape(trial_block.shape)
    potentials = jnp.dot(inverse, flat_p, precision=high).reshape(trial_block.shape)
    return (rotated, potentials, ritz_matrix)
```

```python
import functools

import jax
import jax.numpy as jnp
import numpy as np
from jax import lax
from jax.experimental import pallas as pl
from jax.experimental.pallas import tpu as pltpu
from jax.sharding import PartitionSpec as P

ITERS = 3


COEFFS = (
    -5369.0 / 1800.0,
    12.0 / 7.0,
    -15.0 / 56.0,
    10.0 / 189.0,
    -1.0 / 112.0,
    2.0 / 1925.0,
    -1.0 / 16632.0,
)


def shifted(value, axis, steps):
    count = lax.axis_size(axis)
    pairs = [(source, (source + steps) % count) for source in range(count)]
    return lax.ppermute(value, axis, pairs)


def with_halo(cells, sides, width):
    for axis, dim in sides:
        count = lax.axis_size(axis)
        head = lax.slice_in_dim(cells, 0, width, axis=dim)
        tail = lax.slice_in_dim(cells, cells.shape[dim] - width, cells.shape[dim], axis=dim)
        cells = jnp.concatenate(
            [
                lax.ppermute(tail, axis, [(i, (i + 1) % count) for i in range(count)]),
                cells,
                lax.ppermute(head, axis, [((i + 1) % count, i) for i in range(count)]),
            ],
            axis=dim,
        )
    return cells


def along_axis(total, padded, axis, length):
    for offset in range(1, 7):
        upper = lax.slice_in_dim(padded, 6 + offset, 6 + offset + length, axis=axis)
        lower = lax.slice_in_dim(padded, 6 - offset, 6 - offset + length, axis=axis)
        total = total + COEFFS[offset] * (upper + lower)
    return total


def operate(field):
    stride = max(lax.axis_size("grid") // 16, 2)
    row_count = field.shape[1]
    col_count = field.shape[2]
    total = 3.0 * COEFFS[0] * field
    below = shifted(field, "grid", stride)
    above = shifted(field, "grid", -stride)
    along_x = jnp.concatenate([below, field, above], axis=1)
    total = along_axis(total, along_x, 1, row_count)
    side_halo = with_halo(field, (("grid", 2),), 6)
    total = along_axis(total, side_halo, 2, col_count)
    along_z = jnp.pad(field, ((0, 0), (0, 0), (0, 0), (6, 6)))
    total = along_axis(total, along_z, 3, field.shape[3])
    return -total


def inner(left, right):
    return jnp.sum(left * right, axis=(1, 2, 3))


def expand(values):
    return values[:, None, None, None]


def two_products(residual, image):
    return lax.psum((inner(residual, residual), inner(residual, image)), "grid")


def finish(gram, cross, cells):
    high = lax.Precision.HIGHEST
    gram = gram / cells
    cross = cross / cells
    lower = jnp.linalg.cholesky(gram)
    inverse = lax.linalg.triangular_solve(
        lower, jnp.eye(gram.shape[0], dtype=jnp.float32), left_side=True, lower=True
    )
    middle = jnp.dot(inverse, 0.5 * (cross + cross.T), precision=high)
    return (inverse, jnp.dot(middle, inverse.T, precision=high))


def body(trial_block, response_weight):
    high = lax.Precision.HIGHEST
    source = response_weight[None] * trial_block
    solution = jnp.zeros_like(source)
    residual = source
    image = operate(residual)
    norm_now, product = two_products(residual, image)
    alpha = norm_now / product
    direction, along = (residual, image)
    for step in range(ITERS):
        solution = solution + expand(alpha) * direction
        residual = residual - expand(alpha) * along
        if step + 1 < ITERS:
            image = operate(residual)
            norm_next, product = two_products(residual, image)
            ratio = norm_next / norm_now
            alpha = norm_next / (product - ratio * norm_next / alpha)
            direction = residual + expand(ratio) * direction
            along = image + expand(ratio) * along
            norm_now = norm_next
    local_count = trial_block.shape[0]
    whole_x, whole_p = (
        lax.all_gather(trial_block, "vec", axis=0, tiled=True),
        lax.all_gather(solution, "vec", axis=0, tiled=True),
    )
    flat_x = whole_x.reshape(whole_x.shape[0], -1)
    flat_p = whole_p.reshape(whole_p.shape[0], -1)
    gram, cross = lax.psum(
        (jnp.dot(flat_x, flat_x.T, precision=high), jnp.dot(flat_x, flat_p.T, precision=high)),
        "grid",
    )
    cells = lax.axis_size("grid") * flat_x.shape[1]
    inverse, ritz_matrix = finish(gram, cross, cells)
    own_rows = lax.dynamic_slice_in_dim(
        inverse, lax.axis_index("vec") * local_count, local_count, 0
    )
    rotated = jnp.dot(own_rows, flat_x, precision=high).reshape(trial_block.shape)
    potentials = jnp.dot(own_rows, flat_p, precision=high).reshape(trial_block.shape)
    return (rotated, potentials, ritz_matrix)


MESH_ID = pl.DeviceIdType.MESH
PAD = 8
HALO = 6
ROUNDS = 4


def split_loss():
    exact = np.array(COEFFS[1:], np.float32)
    high = exact.astype(jnp.bfloat16).astype(np.float32)
    low = (exact - high).astype(jnp.bfloat16).astype(np.float32)
    return float(2.0 * np.sum(exact.astype(np.float64) - high - low))


CENTRE = 3.0 * COEFFS[0] + split_loss()


def kernel(
    groups, parts, trial, weight, rotated, potentials, ritz,
    wbuf, src, res, res1, res2, img, img1, phi, band, held, waves, gmsg, gin, cmsg, cin, mats, coef,
    near, fsend, frecv, tsend, trecv, rsend, rrecv, bsend, brecv, psend, precv, xsend, xrecv,
    ysend, yrecv, gsend, grecv, csend, crecv, isend,
):
    nl, rows, cols, depth = trial.shape
    nvec = parts * nl
    blocks = groups // 2
    mid = blocks // 2
    length = blocks * rows
    wide_y = 2 * cols
    total_devices = groups * parts
    f32, bf16 = jnp.float32, jnp.bfloat16
    me_g = lax.axis_index("grid")
    me_v = lax.axis_index("vec")
    me = me_g * parts + me_v
    z, y = lax.div(me_g, 2), lax.rem(me_g, 2)
    x, c = lax.div(me_v, 2), lax.rem(me_v, 2)
    center = slice(PAD, PAD + wide_y)

    def place(pz, py, px, pc):
        return (pz * 2 + py, px * 2 + pc)

    partner = place(z, y, x, 1 - c)
    barrier = pltpu.get_barrier_semaphore()

    def greet(sem, device):
        pl.semaphore_signal(sem, inc=1, device_id=device, device_id_type=MESH_ID)

    def around(sem, cores):
        for core in cores:
            greet(sem, place(z, y, 1 - x, core))
            greet(sem, place(z, 1 - y, x, core))

            @pl.when(z > 0)
            def _():
                greet(sem, place(z - 1, y, x, core))

            @pl.when(z < blocks - 1)
            def _():
                greet(sem, place(z + 1, y, x, core))

    sides = 4 - jnp.where(z > 0, 0, 1) - jnp.where(z < blocks - 1, 0, 1)
    greet(barrier, partner)
    around(barrier, (c, 1 - c))

    fetches = [
        pltpu.make_async_copy(weight, wbuf, isend.at[0]),
        pltpu.make_async_copy(trial, held.at[pl.ds(me_v * nl, nl)], isend.at[1]),
    ]
    for fetch in fetches:
        fetch.start()

    row_id = lax.broadcasted_iota(jnp.int32, (depth, depth), 0)
    gap = jnp.abs(row_id - lax.broadcasted_iota(jnp.int32, (depth, depth), 1))
    taps = jnp.zeros((depth, depth), f32)
    for k in range(1, HALO + 1):
        taps = jnp.where(gap == k, COEFFS[k], taps)
    taps_high = taps.astype(bf16)
    taps_low = (taps - taps_high.astype(f32)).astype(bf16)
    band[0:depth, 0:depth] = taps_high
    band[depth:, 0:depth] = taps_high
    band[0:depth, depth:] = taps_low
    band[depth:, depth:] = taps_low

    for fetch in fetches:
        fetch.wait()

    def prepare(i, carry):
        scale = wbuf[i]
        for s in range(nl):
            src[s, i] = scale * held[me_v * nl + s, i]
        return carry

    lax.fori_loop(0, rows, prepare, 0)
    pl.semaphore_wait(barrier, 1 + 2 * sides)

    def remote(source, target, send, recv, device):
        return pltpu.make_async_remote_copy(
            src_ref=source, dst_ref=target, send_sem=send, recv_sem=recv,
            device_id=device, device_id_type=MESH_ID,
        )

    def slab(bz, by):
        return res.at[pl.ds(bz * rows, rows), pl.ds(pl.multiple_of(PAD + by * cols, PAD), cols)]

    def host_of(s):
        return (mid - 1 + c, s % 2, x, s // 2)

    def own_slot(s):
        hz, hy, _, hc = host_of(s)
        return jnp.logical_and(jnp.logical_and(hz == z, hy == y), hc == c)

    def hops(s):
        hz, hy, _, _ = host_of(s)
        return jnp.abs(hz - z) + jnp.abs(hy - y)

    def forward(s):
        return remote(src.at[s], slab(z, y), fsend.at[s], frecv.at[me_g], place(*host_of(s)))

    def send_forward(s, test):
        @pl.when(jnp.logical_and(test, jnp.logical_not(own_slot(s))))
        def _():
            forward(s).start()

    def slot_ref(buffer, v):
        return buffer.at[pl.ds(v * nl, nl)]

    own_trial = slot_ref(held, me_v)
    trial_copies = [
        remote(own_trial, own_trial, tsend.at[0], trecv.at[0], partner),
        remote(own_trial, own_trial, tsend.at[1], trecv.at[1 + c], place(z, y, 1 - x, 0)),
    ]

    def trial_arrival(core):
        slot = slot_ref(held, (1 - x) * 2 + core)
        return remote(slot, slot, tsend.at[1], trecv.at[1 + core], partner)

    def trial_relay(core):
        slot = slot_ref(held, (1 - x) * 2 + core)
        return remote(slot, slot, rsend.at[core], rrecv.at[core], partner)

    around(near.at[0], (c,))
    for s in range(nl // 2):
        send_forward(s, hops(s) <= 1)
    trial_copies[1].start()
    trial_copies[0].start()
    for reach in range(2, ROUNDS + 2):
        pl.semaphore_wait(near.at[reach - 2], sides)
        if reach < ROUNDS + 1:
            around(near.at[reach - 1], (c,))
        if reach == 2:
            for s in range(nl // 2):
                send_forward(s, hops(s) == 2)
        if reach == 3:
            for s in range(nl // 2):
                send_forward(s, hops(s) > 2)
            for s in range(nl // 2, nl):
                send_forward(s, hops(s) >= 0)

    for s in range(nl):
        @pl.when(own_slot(s))
        def _():
            res[pl.ds(z * rows, rows), pl.ds(pl.multiple_of(PAD + y * cols, PAD), cols)] = src[s]

    hosted_c = z - (mid - 1)
    hosted_s = c * 2 + y
    hosted_v = x * 2 + hosted_c
    hosts = jnp.logical_and(z >= mid - 1, z <= mid)

    def along_depth(value):
        high = value.astype(bf16)
        low = (value - high.astype(f32)).astype(bf16)
        both = jnp.dot(
            jnp.concatenate([high, low], axis=1), band[...], preferred_element_type=f32
        )
        return both[:, :depth] + both[:, depth:]

    def folded(value):
        return value.reshape(wide_y // 8, 8, depth).sum(axis=0)

    def full(value):
        return jnp.sum(value, axis=(0, 1), keepdims=True)

    def wide(value):
        return jnp.broadcast_to(value, (wide_y, depth))

    def sweep(one, start):
        return lax.fori_loop(0, length, one, start, unroll=length)

    zero = jnp.zeros((8, depth), f32)

    def wrap(field, i, value):
        field[lax.rem(i + rows, length), 0:PAD] = value[wide_y - PAD :]
        field[lax.rem(i + length - rows, length), PAD + wide_y :] = value[:PAD]

    def operate(field, image):
        def one(i, carry):
            norm, product = carry
            value = field[i, center]
            acc = CENTRE * value + along_depth(value)
            for k in range(1, HALO + 1):
                beside = field[lax.rem(i + k, length), center]
                beside = beside + field[lax.rem(i + length - k, length), center]
                across = field[i, PAD + k : PAD + k + wide_y] + field[i, PAD - k : PAD - k + wide_y]
                acc = acc + COEFFS[k] * (beside + across)
            acc = -acc
            image[i] = acc
            return (norm + folded(value * value), product + folded(value * acc))

        norm, product = sweep(one, (zero, zero))
        return full(norm), full(product)

    def energy(field):
        def one(i, carry):
            norm, product = carry
            value = field[i, center]
            acc = (0.5 * CENTRE) * value + 0.5 * along_depth(value)
            for k in range(1, HALO + 1):
                ahead = field[lax.rem(i + k, length), center]
                acc = acc + COEFFS[k] * (ahead + field[i, PAD + k : PAD + k + wide_y])
            return (norm + folded(value * value), product + folded(value * acc))

        norm, product = sweep(one, (zero, zero))
        return full(norm), -2.0 * full(product)

    def back(order, by):
        bz = order + hosted_c * (blocks - 1 - 2 * order)
        return bz, remote(
            phi.at[pl.ds(bz * rows, rows), by * cols : (by + 1) * cols],
            waves.at[hosted_v * nl + hosted_s],
            bsend.at[order * 2 + by], brecv.at[hosted_s], place(bz, by, x, hosted_c),
        )

    def kept(bz, by):
        return jnp.logical_and(jnp.logical_and(bz == z, by == y), hosted_c == c)

    orders = list(range(blocks - 1, mid - 1, -1)) + list(range(mid))

    @pl.when(hosts)
    def _():
        for bg in range(groups):
            @pl.when(jnp.logical_not(jnp.logical_and(bg == me_g, hosted_c == c)))
            def _():
                remote(
                    src.at[0], slab(bg // 2, bg % 2), fsend.at[0], frecv.at[bg], partner
                ).wait_recv()

        def fill(i, carry):
            field = res
            field[lax.rem(i + rows, length), 0:PAD] = field[i, wide_y : wide_y + PAD]
            field[lax.rem(i + length - rows, length), PAD + wide_y :] = field[i, PAD : 2 * PAD]
            return carry

        sweep(fill, 0)
        norm, product = operate(res, img)
        alpha = norm / product
        alpha_wide = wide(alpha)

        def first(i, carry):
            value = res[i, center] - alpha_wide * img[i]
            res1[i, center] = value
            wrap(res1, i, value)
            return carry

        sweep(first, 0)
        norm1, product = operate(res1, img1)
        ratio1 = norm1 / norm
        alpha1 = norm1 / (product - ratio1 * norm1 / alpha)
        image1_wide, image0_wide = wide(alpha1), wide(alpha1 * ratio1)

        def second(i, carry):
            value = res1[i, center] - image1_wide * img1[i] - image0_wide * img[i]
            res2[i, center] = value
            wrap(res2, i, value)
            return carry

        sweep(second, 0)
        norm2, product = energy(res2)
        ratio2 = norm2 / norm1
        alpha2 = norm2 / (product - ratio2 * norm2 / alpha1)
        share1 = alpha1 + alpha2 * ratio2
        share0 = wide(alpha + share1 * ratio1)
        share1 = wide(share1)
        share2 = wide(alpha2)
        for order in orders:
            bz = order + hosted_c * (blocks - 1 - 2 * order)

            def last(i, carry):
                row = bz * rows + i
                phi[row] = (
                    share0 * res[row, center] + share1 * res1[row, center] + share2 * res2[row, center]
                )
                return carry

            lax.fori_loop(0, rows, last, 0, unroll=rows)
            for by in range(2):
                _, copy = back(order, by)

                @pl.when(jnp.logical_not(kept(bz, by)))
                def _():
                    copy.start()

                @pl.when(kept(bz, by))
                def _():
                    waves[hosted_v * nl + hosted_s] = phi[
                        pl.ds(bz * rows, rows), by * cols : (by + 1) * cols
                    ]

    def products(buffer, base, slots):
        lane_row = lax.broadcasted_iota(jnp.int32, (len(slots), depth), 1)

        def one(j, acc):
            other = held[j]
            parts_of = [
                jnp.sum(jnp.sum(buffer[base + s] * other, axis=0), axis=0, keepdims=True)
                for s in slots
            ]
            value = jnp.sum(jnp.concatenate(parts_of, axis=0), axis=1, keepdims=True)
            return jnp.where(lane_row == j, value, acc)

        return lax.fori_loop(0, nvec, one, jnp.zeros((len(slots), depth), f32), unroll=4)

    def device_at(k):
        target = lax.rem(me + k, total_devices)
        return (lax.div(target, parts), lax.rem(target, parts))

    def spread(message, slot, send, recv):
        def start(k, carry):
            remote(message, slot, send.at[k], recv, device_at(k)).start()
            return carry

        lax.fori_loop(1, total_devices, start, 0)

    def drain(message, slot, send, recv):
        def wait(k, carry):
            remote(message, slot, send.at[k], recv, device_at(k)).wait_send()
            return carry

        lax.fori_loop(1, total_devices, wait, 0)

    gram_slot, gram_recv = gin.at[me_g * 2 + x], grecv.at[me_g * 2 + x]

    trial_copies[0].wait_recv()

    @pl.when(c == 0)
    def _():
        for core in range(2):
            trial_arrival(core).wait_recv()
            trial_relay(core).start()
        gmsg[...] = products(held, x * 2 * nl, range(2 * nl))
        gin[me_g * 2 + x] = gmsg[...]
        spread(gmsg, gram_slot, gsend, gram_recv)

    @pl.when(c == 1)
    def _():
        for core in range(2):
            trial_relay(core).wait_recv()

    def wave_over(s):
        slot = waves.at[me_v * nl + s]
        return remote(slot, slot, xsend.at[s], xrecv.at[s], place(z, y, 1, c))

    def wave_core(s):
        slot = waves.at[me_v * nl + s]
        return remote(slot, slot, psend.at[s], precv.at[s], partner)

    def wave_relay(s):
        slot = waves.at[c * nl + s]
        return remote(slot, slot, ysend.at[s], yrecv.at[s], partner)

    def take(s):
        @pl.when(jnp.logical_not(own_slot(s)))
        def _():
            slot = waves.at[me_v * nl + s]
            remote(slot, slot, bsend.at[0], brecv.at[s], partner).wait_recv()

        @pl.when(x == 0)
        def _():
            wave_over(s).start()

        @pl.when(c == 0)
        def _():
            wave_core(s).start()

    def pass_on(s):
        slot = waves.at[c * nl + s]
        remote(slot, slot, xsend.at[s], xrecv.at[s], partner).wait_recv()
        wave_relay(s).start()

    first_half, last_half = range(nl // 2), range(nl // 2, nl)
    for s in first_half:
        take(s)
    cmsg[: nl // 2] = products(waves, me_v * nl, first_half)

    def gather_gram(i, carry):
        owner = lax.rem(i, 2) * 2 + lax.div(i, 2) * parts

        @pl.when(owner != me)
        def _():
            remote(gmsg, gin.at[i], gsend.at[0], grecv.at[i], partner).wait_recv()

        return carry

    lax.fori_loop(0, groups * 2, gather_gram, 0)
    cells = groups * rows * cols * depth
    for px in range(2):
        total = gin[px]
        for g in range(1, groups):
            total = total + gin[g * 2 + px]
        mats[0, px * 2 * nl : (px + 1) * 2 * nl] = total / cells
    gram = mats[0]
    row_of = lax.broadcasted_iota(jnp.int32, (nvec, depth), 0)
    lane_of = lax.broadcasted_iota(jnp.int32, (nvec, depth), 1)
    inverse = jnp.where(row_of == lane_of, 1.0, 0.0)
    for k in range(nvec):
        scale = 1.0 / jnp.sqrt(gram[k : k + 1, k : k + 1])
        column = gram[:, k : k + 1] * scale
        line = inverse[k : k + 1] * scale
        inverse = jnp.where(row_of > k, inverse - column * line, jnp.where(row_of == k, line, inverse))
        gram = gram - column * (gram[k : k + 1] * scale)
    mats[1] = inverse
    own_rows = mats[1, pl.ds(me_v * nl, nl)]
    for i in range(nvec):
        coef[i] = jnp.broadcast_to(own_rows[:, i : i + 1], (nl, depth))

    def rotate(buffer, out, base, count, fresh):
        def one(row, carry):
            totals = [None if fresh else out[s, row] for s in range(nl)]
            for i in range(count):
                value = buffer[base + i, row]
                for s in range(nl):
                    term = coef[base + i, s : s + 1] * value
                    totals[s] = term if totals[s] is None else totals[s] + term
            for s in range(nl):
                out[s, row] = totals[s]
            return carry

        lax.fori_loop(0, rows, one, 0)

    rotate(held, rotated, 0, nvec, True)

    @pl.when(x == 1)
    def _():
        for s in first_half:
            pass_on(s)

    for s in last_half:
        take(s)
    cmsg[nl // 2 :] = products(waves, me_v * nl, last_half)
    cin[me] = cmsg[...]
    cross_slot, cross_recv = cin.at[me], crecv.at[me]
    spread(cmsg, cross_slot, csend, cross_recv)
    rotate(waves, potentials, me_v * nl, nl, True)

    @pl.when(x == 1)
    def _():
        for s in last_half:
            pass_on(s)

    @pl.when(c == 1)
    def _():
        for s in range(nl):
            slot = waves.at[x * 2 * nl + s]
            remote(slot, slot, psend.at[s], precv.at[s], partner).wait_recv()
        rotate(waves, potentials, x * 2 * nl, nl, False)

    @pl.when(x == 1)
    def _():
        rotate(waves, potentials, c * nl, nl, False)
        for s in range(nl):
            slot = waves.at[(1 - c) * nl + s]
            remote(slot, slot, ysend.at[s], yrecv.at[s], partner).wait_recv()
        rotate(waves, potentials, (1 - c) * nl, nl, False)

    def gather_cross(i, carry):
        @pl.when(i != me)
        def _():
            remote(cmsg, cin.at[i], csend.at[0], crecv.at[i], partner).wait_recv()

        return carry

    lax.fori_loop(0, total_devices, gather_cross, 0)
    for v in range(parts):
        total = cin[v]
        for g in range(1, groups):
            total = total + cin[g * parts + v]
        mats[2, v * nl : (v + 1) * nl] = total / cells
    cross = mats[2]
    high = lax.Precision.HIGHEST
    last_dims = (((1,), (1,)), ((), ()))
    inverse = mats[1]
    small = inverse[:, :nvec]
    middle = 0.5 * (
        jnp.dot(small, cross, precision=high)[:, :nvec]
        + lax.dot_general(inverse, cross, last_dims, precision=high)
    )
    ritz[...] = lax.dot_general(middle, small, last_dims, precision=high)

    for s in range(nl):
        @pl.when(jnp.logical_not(own_slot(s)))
        def _():
            forward(s).wait_send()

        @pl.when(x == 0)
        def _():
            wave_over(s).wait_send()

        @pl.when(c == 0)
        def _():
            wave_core(s).wait_send()

        @pl.when(x == 1)
        def _():
            wave_relay(s).wait_send()

    @pl.when(hosts)
    def _():
        for order in orders:
            for by in range(2):
                bz, copy = back(order, by)

                @pl.when(jnp.logical_not(kept(bz, by)))
                def _():
                    copy.wait_send()

    for copy in trial_copies:
        copy.wait_send()

    @pl.when(c == 0)
    def _():
        for core in range(2):
            trial_relay(core).wait_send()
        drain(gmsg, gram_slot, gsend, gram_recv)

    drain(cmsg, cross_slot, csend, cross_recv)


def hosted_body(trial_block, response_weight):
    nl, rows, cols, depth = trial_block.shape
    groups, parts = lax.axis_size("grid"), lax.axis_size("vec")
    nvec, blocks = parts * nl, groups // 2
    length, wide_y, devices = blocks * rows, 2 * cols, groups * parts
    f32 = jnp.float32
    dma = pltpu.SemaphoreType.DMA
    vmem = pl.BlockSpec(memory_space=pltpu.VMEM)
    field = pltpu.VMEM((length, wide_y, depth), f32)
    padded = pltpu.VMEM((length, wide_y + 2 * PAD, depth), f32)
    whole = pltpu.VMEM((nvec, rows, cols, depth), f32)
    return pl.pallas_call(
        functools.partial(kernel, groups, parts),
        out_shape=(
            pltpu.VMEM(trial_block.shape, f32),
            pltpu.VMEM(trial_block.shape, f32),
            pltpu.VMEM((nvec, nvec), f32),
        ),
        in_specs=[pl.BlockSpec(memory_space=pl.ANY)] * 2,
        out_specs=(vmem, vmem, vmem),
        scratch_shapes=[
            pltpu.VMEM((rows, cols, depth), f32),
            pltpu.VMEM((nl, rows, cols, depth), f32),
            padded, padded, padded, field, field, field,
            pltpu.VMEM((2 * depth, 2 * depth), jnp.bfloat16), whole, whole,
            pltpu.VMEM((2 * nl, depth), f32), pltpu.VMEM((2 * groups, 2 * nl, depth), f32),
            pltpu.VMEM((nl, depth), f32), pltpu.VMEM((devices, nl, depth), f32),
            pltpu.VMEM((3, nvec, depth), f32), pltpu.VMEM((nvec, nl, depth), f32),
            pltpu.SemaphoreType.REGULAR((ROUNDS,)),
            dma((nl,)), dma((groups,)), dma((2,)), dma((3,)), dma((2,)), dma((2,)),
            dma((groups,)), dma((nl,)), dma((nl,)), dma((nl,)), dma((nl,)), dma((nl,)),
            dma((nl,)), dma((nl,)),
            dma((devices,)), dma((2 * groups,)), dma((devices,)), dma((devices,)), dma((2,)),
        ],
        compiler_params=pltpu.CompilerParams(collective_id=0, has_side_effects=True),
    )(trial_block, response_weight)


def chosen_body(trial_block, response_weight):
    nl, rows, cols, depth = trial_block.shape
    groups, parts = lax.axis_size("grid"), lax.axis_size("vec")
    fits = (
        max(groups // 16, 2) == 2 and groups == 2 * nl and parts == nl and groups == 2 * ROUNDS
        and rows == HALO and cols % 8 == 0 and cols >= PAD and parts * nl <= depth
    )
    return (hosted_body if fits else body)(trial_block, response_weight)


def solution(mesh):
    placed = (P("vec", "grid", None, None), P("grid", None, None))
    return jax.shard_map(
        chosen_body,
        mesh=mesh,
        in_specs=placed,
        out_specs=(P("vec", "grid", None, None), P("vec", "grid", None, None), P()),
        check_vma=False,
    )
```

```python
import functools

import jax
import jax.numpy as jnp
import numpy as np
from jax import lax
from jax.experimental import pallas as pl
from jax.experimental.pallas import tpu as pltpu
from jax.sharding import PartitionSpec as P

ITERS = 3


COEFFS = (
    -5369.0 / 1800.0,
    12.0 / 7.0,
    -15.0 / 56.0,
    10.0 / 189.0,
    -1.0 / 112.0,
    2.0 / 1925.0,
    -1.0 / 16632.0,
)


def shifted(value, axis, steps):
    count = lax.axis_size(axis)
    pairs = [(source, (source + steps) % count) for source in range(count)]
    return lax.ppermute(value, axis, pairs)


def with_halo(cells, sides, width):
    for axis, dim in sides:
        count = lax.axis_size(axis)
        head = lax.slice_in_dim(cells, 0, width, axis=dim)
        tail = lax.slice_in_dim(cells, cells.shape[dim] - width, cells.shape[dim], axis=dim)
        cells = jnp.concatenate(
            [
                lax.ppermute(tail, axis, [(i, (i + 1) % count) for i in range(count)]),
                cells,
                lax.ppermute(head, axis, [((i + 1) % count, i) for i in range(count)]),
            ],
            axis=dim,
        )
    return cells


def along_axis(total, padded, axis, length):
    for offset in range(1, 7):
        upper = lax.slice_in_dim(padded, 6 + offset, 6 + offset + length, axis=axis)
        lower = lax.slice_in_dim(padded, 6 - offset, 6 - offset + length, axis=axis)
        total = total + COEFFS[offset] * (upper + lower)
    return total


def operate(field):
    stride = max(lax.axis_size("grid") // 16, 2)
    row_count = field.shape[1]
    col_count = field.shape[2]
    total = 3.0 * COEFFS[0] * field
    below = shifted(field, "grid", stride)
    above = shifted(field, "grid", -stride)
    along_x = jnp.concatenate([below, field, above], axis=1)
    total = along_axis(total, along_x, 1, row_count)
    side_halo = with_halo(field, (("grid", 2),), 6)
    total = along_axis(total, side_halo, 2, col_count)
    along_z = jnp.pad(field, ((0, 0), (0, 0), (0, 0), (6, 6)))
    total = along_axis(total, along_z, 3, field.shape[3])
    return -total


def inner(left, right):
    return jnp.sum(left * right, axis=(1, 2, 3))


def expand(values):
    return values[:, None, None, None]


def two_products(residual, image):
    return lax.psum((inner(residual, residual), inner(residual, image)), "grid")


def finish(gram, cross, cells):
    high = lax.Precision.HIGHEST
    gram = gram / cells
    cross = cross / cells
    lower = jnp.linalg.cholesky(gram)
    inverse = lax.linalg.triangular_solve(
        lower, jnp.eye(gram.shape[0], dtype=jnp.float32), left_side=True, lower=True
    )
    middle = jnp.dot(inverse, 0.5 * (cross + cross.T), precision=high)
    return (inverse, jnp.dot(middle, inverse.T, precision=high))


def body(trial_block, response_weight):
    high = lax.Precision.HIGHEST
    source = response_weight[None] * trial_block
    solution = jnp.zeros_like(source)
    residual = source
    image = operate(residual)
    norm_now, product = two_products(residual, image)
    alpha = norm_now / product
    direction, along = (residual, image)
    for step in range(ITERS):
        solution = solution + expand(alpha) * direction
        residual = residual - expand(alpha) * along
        if step + 1 < ITERS:
            image = operate(residual)
            norm_next, product = two_products(residual, image)
            ratio = norm_next / norm_now
            alpha = norm_next / (product - ratio * norm_next / alpha)
            direction = residual + expand(ratio) * direction
            along = image + expand(ratio) * along
            norm_now = norm_next
    local_count = trial_block.shape[0]
    whole_x, whole_p = (
        lax.all_gather(trial_block, "vec", axis=0, tiled=True),
        lax.all_gather(solution, "vec", axis=0, tiled=True),
    )
    flat_x = whole_x.reshape(whole_x.shape[0], -1)
    flat_p = whole_p.reshape(whole_p.shape[0], -1)
    gram, cross = lax.psum(
        (jnp.dot(flat_x, flat_x.T, precision=high), jnp.dot(flat_x, flat_p.T, precision=high)),
        "grid",
    )
    cells = lax.axis_size("grid") * flat_x.shape[1]
    inverse, ritz_matrix = finish(gram, cross, cells)
    own_rows = lax.dynamic_slice_in_dim(
        inverse, lax.axis_index("vec") * local_count, local_count, 0
    )
    rotated = jnp.dot(own_rows, flat_x, precision=high).reshape(trial_block.shape)
    potentials = jnp.dot(own_rows, flat_p, precision=high).reshape(trial_block.shape)
    return (rotated, potentials, ritz_matrix)


MESH_ID = pl.DeviceIdType.MESH
PAD = 8
HALO = 6


def split_loss():
    exact = np.array(COEFFS[1:], np.float32)
    high = exact.astype(jnp.bfloat16).astype(np.float32)
    low = (exact - high).astype(jnp.bfloat16).astype(np.float32)
    return float(2.0 * np.sum(exact.astype(np.float64) - high - low))


CENTRE = 3.0 * COEFFS[0] + split_loss()


def kernel(
    groups, parts, trial, weight, rotated, potentials, ritz,
    wbuf, src, res, res1, res2, img, img1, phi, band, held, waves, gmsg, gin, cmsg, cin, mats, coef,
    near, fsend, frecv, tsend, trecv, rsend, rrecv, bsend, brecv, psend, precv, xsend, xrecv,
    ysend, yrecv, gsend, grecv, csend, crecv, isend,
):
    nl, rows, cols, depth = trial.shape
    nvec = parts * nl
    blocks = groups // 2
    mid = blocks // 2
    length = blocks * rows
    wide_y = 2 * cols
    total_devices = groups * parts
    f32, bf16 = jnp.float32, jnp.bfloat16
    me_g = lax.axis_index("grid")
    me_v = lax.axis_index("vec")
    me = me_g * parts + me_v
    z, y = lax.div(me_g, 2), lax.rem(me_g, 2)
    x, c = lax.div(me_v, 2), lax.rem(me_v, 2)
    center = slice(PAD, PAD + wide_y)

    def place(pz, py, px, pc):
        return (pz * 2 + py, px * 2 + pc)

    partner = place(z, y, x, 1 - c)
    barrier = pltpu.get_barrier_semaphore()

    def greet(sem, device):
        pl.semaphore_signal(sem, inc=1, device_id=device, device_id_type=MESH_ID)

    within = 0
    for step in range(1, groups):
        for core in range(2):
            there = lax.rem(me_g + step, groups)
            far = jnp.abs(lax.div(there, 2) - z) + jnp.abs(lax.rem(there, 2) - y) > 3
            within = within + jnp.where(far, 0, 1)

            @pl.when(jnp.logical_not(far))
            def _():
                greet(barrier, (there, x * 2 + core))

    greet(barrier, partner)
    for core in range(2):
        greet(barrier, place(z, y, 1 - x, core))
    greet(barrier, place(z, 1 - y, 1 - x, c))

    fetches = [
        pltpu.make_async_copy(weight, wbuf, isend.at[0]),
        pltpu.make_async_copy(trial, held.at[pl.ds(me_v * nl, nl)], isend.at[1]),
    ]
    for fetch in fetches:
        fetch.start()

    row_id = lax.broadcasted_iota(jnp.int32, (depth, depth), 0)
    gap = jnp.abs(row_id - lax.broadcasted_iota(jnp.int32, (depth, depth), 1))
    taps = jnp.zeros((depth, depth), f32)
    for k in range(1, HALO + 1):
        taps = jnp.where(gap == k, COEFFS[k], taps)
    taps_high = taps.astype(bf16)
    taps_low = (taps - taps_high.astype(f32)).astype(bf16)
    band[0:depth, 0:depth] = taps_high
    band[depth:, 0:depth] = taps_high
    band[0:depth, depth:] = taps_low
    band[depth:, depth:] = taps_low

    for fetch in fetches:
        fetch.wait()

    def prepare(i, carry):
        scale = wbuf[i]
        for s in range(nl):
            src[s, i] = scale * held[me_v * nl + s, i]
        return carry

    lax.fori_loop(0, rows, prepare, 0)
    pl.semaphore_wait(barrier, within + 4)

    def remote(source, target, send, recv, device):
        return pltpu.make_async_remote_copy(
            src_ref=source, dst_ref=target, send_sem=send, recv_sem=recv,
            device_id=device, device_id_type=MESH_ID,
        )

    def slab(bz, by):
        return res.at[pl.ds(bz * rows, rows), pl.ds(pl.multiple_of(PAD + by * cols, PAD), cols)]

    def host_of(s):
        return (mid - 1 + c, s % 2, x, s // 2)

    def own_slot(s):
        hz, hy, _, hc = host_of(s)
        return jnp.logical_and(jnp.logical_and(hz == z, hy == y), hc == c)

    def forward(s):
        return remote(src.at[s], slab(z, y), fsend.at[s], frecv.at[me_g], place(*host_of(s)))

    def send_forward(s):
        @pl.when(jnp.logical_not(own_slot(s)))
        def _():
            forward(s).start()

    def slot_ref(buffer, v):
        return buffer.at[pl.ds(v * nl, nl)]

    own_trial = slot_ref(held, me_v)
    trial_copies = [
        remote(own_trial, own_trial, tsend.at[0], trecv.at[0], partner),
        remote(own_trial, own_trial, tsend.at[1], trecv.at[1 + c], place(z, y, 1 - x, 0)),
    ]

    def trial_arrival(core):
        slot = slot_ref(held, (1 - x) * 2 + core)
        return remote(slot, slot, tsend.at[1], trecv.at[1 + core], partner)

    def trial_relay(core):
        slot = slot_ref(held, (1 - x) * 2 + core)
        return remote(slot, slot, rsend.at[core], rrecv.at[core], partner)

    for s in range(nl):
        send_forward(s)
    trial_copies[1].start()
    trial_copies[0].start()
    for device in (place(z, 1 - y, x, c), place(z, y, 1 - x, c), place(z, 1 - y, 1 - x, c)):
        greet(near.at[0], device)
    for s in range(nl):
        @pl.when(own_slot(s))
        def _():
            res[pl.ds(z * rows, rows), pl.ds(pl.multiple_of(PAD + y * cols, PAD), cols)] = src[s]

    pl.semaphore_wait(near.at[0], 3)

    hosted_c = z - (mid - 1)
    hosted_s = c * 2 + y
    hosted_v = x * 2 + hosted_c
    hosts = jnp.logical_and(z >= mid - 1, z <= mid)

    def along_depth(value):
        high = value.astype(bf16)
        low = (value - high.astype(f32)).astype(bf16)
        both = jnp.dot(
            jnp.concatenate([high, low], axis=1), band[...], preferred_element_type=f32
        )
        return both[:, :depth] + both[:, depth:]

    def folded(value):
        return value.reshape(wide_y // 8, 8, depth).sum(axis=0)

    def full(value):
        return jnp.sum(value, axis=(0, 1), keepdims=True)

    def wide(value):
        return jnp.broadcast_to(value, (wide_y, depth))

    def sweep(one, start):
        return lax.fori_loop(0, length, one, start, unroll=length)

    zero = jnp.zeros((8, depth), f32)

    def wrap(field, i, value):
        field[lax.rem(i + rows, length), 0:PAD] = value[wide_y - PAD :]
        field[lax.rem(i + length - rows, length), PAD + wide_y :] = value[:PAD]

    def operate(field, image):
        def one(i, carry):
            norm, product = carry
            value = field[i, center]
            acc = CENTRE * value + along_depth(value)
            for k in range(1, HALO + 1):
                beside = field[lax.rem(i + k, length), center]
                beside = beside + field[lax.rem(i + length - k, length), center]
                across = field[i, PAD + k : PAD + k + wide_y] + field[i, PAD - k : PAD - k + wide_y]
                acc = acc + COEFFS[k] * (beside + across)
            acc = -acc
            image[i] = acc
            return (norm + folded(value * value), product + folded(value * acc))

        norm, product = sweep(one, (zero, zero))
        return full(norm), full(product)

    def energy(field):
        def one(i, carry):
            norm, product = carry
            value = field[i, center]
            acc = (0.5 * CENTRE) * value + 0.5 * along_depth(value)
            for k in range(1, HALO + 1):
                ahead = field[lax.rem(i + k, length), center]
                acc = acc + COEFFS[k] * (ahead + field[i, PAD + k : PAD + k + wide_y])
            return (norm + folded(value * value), product + folded(value * acc))

        norm, product = sweep(one, (zero, zero))
        return full(norm), -2.0 * full(product)

    def back(order, by):
        bz = order + hosted_c * (blocks - 1 - 2 * order)
        return bz, remote(
            phi.at[pl.ds(bz * rows, rows), by * cols : (by + 1) * cols],
            waves.at[hosted_v * nl + hosted_s],
            bsend.at[order * 2 + by], brecv.at[hosted_s], place(bz, by, x, hosted_c),
        )

    def kept(bz, by):
        return jnp.logical_and(jnp.logical_and(bz == z, by == y), hosted_c == c)

    orders = list(range(blocks - 1, mid - 1, -1)) + list(range(mid))

    @pl.when(hosts)
    def _():
        for bg in range(groups):
            @pl.when(jnp.logical_not(jnp.logical_and(bg == me_g, hosted_c == c)))
            def _():
                remote(
                    src.at[0], slab(bg // 2, bg % 2), fsend.at[0], frecv.at[bg], partner
                ).wait_recv()

        def fill(i, carry):
            field = res
            field[lax.rem(i + rows, length), 0:PAD] = field[i, wide_y : wide_y + PAD]
            field[lax.rem(i + length - rows, length), PAD + wide_y :] = field[i, PAD : 2 * PAD]
            return carry

        sweep(fill, 0)
        norm, product = operate(res, img)
        alpha = norm / product
        alpha_wide = wide(alpha)

        def first(i, carry):
            value = res[i, center] - alpha_wide * img[i]
            res1[i, center] = value
            wrap(res1, i, value)
            return carry

        sweep(first, 0)
        norm1, product = operate(res1, img1)
        ratio1 = norm1 / norm
        alpha1 = norm1 / (product - ratio1 * norm1 / alpha)
        image1_wide, image0_wide = wide(alpha1), wide(alpha1 * ratio1)

        def second(i, carry):
            value = res1[i, center] - image1_wide * img1[i] - image0_wide * img[i]
            res2[i, center] = value
            wrap(res2, i, value)
            return carry

        sweep(second, 0)
        norm2, product = energy(res2)
        ratio2 = norm2 / norm1
        alpha2 = norm2 / (product - ratio2 * norm2 / alpha1)
        share1 = alpha1 + alpha2 * ratio2
        share0 = wide(alpha + share1 * ratio1)
        share1 = wide(share1)
        share2 = wide(alpha2)
        for order in orders:
            bz = order + hosted_c * (blocks - 1 - 2 * order)

            def last(i, carry):
                row = bz * rows + i
                phi[row] = (
                    share0 * res[row, center] + share1 * res1[row, center] + share2 * res2[row, center]
                )
                return carry

            lax.fori_loop(0, rows, last, 0, unroll=rows)
            for by in range(2):
                _, copy = back(order, by)

                @pl.when(jnp.logical_not(kept(bz, by)))
                def _():
                    copy.start()

                @pl.when(kept(bz, by))
                def _():
                    waves[hosted_v * nl + hosted_s] = phi[
                        pl.ds(bz * rows, rows), by * cols : (by + 1) * cols
                    ]

    def products(buffer, base, slots):
        lane_row = lax.broadcasted_iota(jnp.int32, (len(slots), depth), 1)

        def one(j, acc):
            other = held[j]
            parts_of = [
                jnp.sum(jnp.sum(buffer[base + s] * other, axis=0), axis=0, keepdims=True)
                for s in slots
            ]
            value = jnp.sum(jnp.concatenate(parts_of, axis=0), axis=1, keepdims=True)
            return jnp.where(lane_row == j, value, acc)

        return lax.fori_loop(0, nvec, one, jnp.zeros((len(slots), depth), f32), unroll=4)

    def device_at(k):
        target = lax.rem(me + k, total_devices)
        return (lax.div(target, parts), lax.rem(target, parts))

    def spread(message, slot, send, recv):
        def start(k, carry):
            remote(message, slot, send.at[k], recv, device_at(k)).start()
            return carry

        lax.fori_loop(1, total_devices, start, 0)

    def drain(message, slot, send, recv):
        def wait(k, carry):
            remote(message, slot, send.at[k], recv, device_at(k)).wait_send()
            return carry

        lax.fori_loop(1, total_devices, wait, 0)

    gram_slot, gram_recv = gin.at[me_g * 2 + x], grecv.at[me_g * 2 + x]

    trial_copies[0].wait_recv()

    @pl.when(c == 0)
    def _():
        for core in range(2):
            trial_arrival(core).wait_recv()
            trial_relay(core).start()
        gmsg[...] = products(held, x * 2 * nl, range(2 * nl))
        gin[me_g * 2 + x] = gmsg[...]
        spread(gmsg, gram_slot, gsend, gram_recv)

    @pl.when(c == 1)
    def _():
        for core in range(2):
            trial_relay(core).wait_recv()

    def wave_over(s):
        slot = waves.at[me_v * nl + s]
        return remote(slot, slot, xsend.at[s], xrecv.at[s], place(z, y, 1, c))

    def wave_core(s):
        slot = waves.at[me_v * nl + s]
        return remote(slot, slot, psend.at[s], precv.at[s], partner)

    def wave_relay(s):
        slot = waves.at[c * nl + s]
        return remote(slot, slot, ysend.at[s], yrecv.at[s], partner)

    def take(s):
        @pl.when(jnp.logical_not(own_slot(s)))
        def _():
            slot = waves.at[me_v * nl + s]
            remote(slot, slot, bsend.at[0], brecv.at[s], partner).wait_recv()

        @pl.when(x == 0)
        def _():
            wave_over(s).start()

        @pl.when(c == 0)
        def _():
            wave_core(s).start()

    def pass_on(s):
        slot = waves.at[c * nl + s]
        remote(slot, slot, xsend.at[s], xrecv.at[s], partner).wait_recv()
        wave_relay(s).start()

    first_half, last_half = range(nl // 2), range(nl // 2, nl)
    for s in first_half:
        take(s)
    cmsg[: nl // 2] = products(waves, me_v * nl, first_half)

    @pl.when(x == 1)
    def _():
        for s in first_half:
            pass_on(s)

    for s in last_half:
        take(s)
    cmsg[nl // 2 :] = products(waves, me_v * nl, last_half)
    cin[me] = cmsg[...]
    cross_slot, cross_recv = cin.at[me], crecv.at[me]
    spread(cmsg, cross_slot, csend, cross_recv)

    def gather_gram(i, carry):
        owner = lax.rem(i, 2) * 2 + lax.div(i, 2) * parts

        @pl.when(owner != me)
        def _():
            remote(gmsg, gin.at[i], gsend.at[0], grecv.at[i], partner).wait_recv()

        return carry

    lax.fori_loop(0, groups * 2, gather_gram, 0)
    cells = groups * rows * cols * depth
    for px in range(2):
        total = gin[px]
        for g in range(1, groups):
            total = total + gin[g * 2 + px]
        mats[0, px * 2 * nl : (px + 1) * 2 * nl] = total / cells
    gram = mats[0]
    row_of = lax.broadcasted_iota(jnp.int32, (nvec, depth), 0)
    lane_of = lax.broadcasted_iota(jnp.int32, (nvec, depth), 1)
    inverse = jnp.where(row_of == lane_of, 1.0, 0.0)
    for k in range(nvec):
        scale = 1.0 / jnp.sqrt(gram[k : k + 1, k : k + 1])
        column = gram[:, k : k + 1] * scale
        line = inverse[k : k + 1] * scale
        inverse = jnp.where(row_of > k, inverse - column * line, jnp.where(row_of == k, line, inverse))
        gram = gram - column * (gram[k : k + 1] * scale)
    mats[1] = inverse
    own_rows = mats[1, pl.ds(me_v * nl, nl)]
    for i in range(nvec):
        coef[i] = jnp.broadcast_to(own_rows[:, i : i + 1], (nl, depth))

    def rotate(buffer, out, base, count, fresh):
        def one(row, carry):
            totals = [None if fresh else out[s, row] for s in range(nl)]
            for i in range(count):
                value = buffer[base + i, row]
                for s in range(nl):
                    term = coef[base + i, s : s + 1] * value
                    totals[s] = term if totals[s] is None else totals[s] + term
            for s in range(nl):
                out[s, row] = totals[s]
            return carry

        lax.fori_loop(0, rows, one, 0)

    rotate(waves, potentials, me_v * nl, nl, True)

    @pl.when(x == 1)
    def _():
        for s in last_half:
            pass_on(s)

    rotate(held, rotated, 0, nvec, True)

    @pl.when(c == 1)
    def _():
        for s in range(nl):
            slot = waves.at[x * 2 * nl + s]
            remote(slot, slot, psend.at[s], precv.at[s], partner).wait_recv()
        rotate(waves, potentials, x * 2 * nl, nl, False)

    @pl.when(x == 1)
    def _():
        rotate(waves, potentials, c * nl, nl, False)
        for s in range(nl):
            slot = waves.at[(1 - c) * nl + s]
            remote(slot, slot, ysend.at[s], yrecv.at[s], partner).wait_recv()
        rotate(waves, potentials, (1 - c) * nl, nl, False)

    def gather_cross(i, carry):
        @pl.when(i != me)
        def _():
            remote(cmsg, cin.at[i], csend.at[0], crecv.at[i], partner).wait_recv()

        return carry

    lax.fori_loop(0, total_devices, gather_cross, 0)
    for v in range(parts):
        total = cin[v]
        for g in range(1, groups):
            total = total + cin[g * parts + v]
        mats[2, v * nl : (v + 1) * nl] = total / cells
    cross = mats[2]
    high = lax.Precision.HIGHEST
    last_dims = (((1,), (1,)), ((), ()))
    inverse = mats[1]
    small = inverse[:, :nvec]
    middle = 0.5 * (
        jnp.dot(small, cross, precision=high)[:, :nvec]
        + lax.dot_general(inverse, cross, last_dims, precision=high)
    )
    ritz[...] = lax.dot_general(middle, small, last_dims, precision=high)

    for s in range(nl):
        @pl.when(jnp.logical_not(own_slot(s)))
        def _():
            forward(s).wait_send()

        @pl.when(x == 0)
        def _():
            wave_over(s).wait_send()

        @pl.when(c == 0)
        def _():
            wave_core(s).wait_send()

        @pl.when(x == 1)
        def _():
            wave_relay(s).wait_send()

    @pl.when(hosts)
    def _():
        for order in orders:
            for by in range(2):
                bz, copy = back(order, by)

                @pl.when(jnp.logical_not(kept(bz, by)))
                def _():
                    copy.wait_send()

    for copy in trial_copies:
        copy.wait_send()

    @pl.when(c == 0)
    def _():
        for core in range(2):
            trial_relay(core).wait_send()
        drain(gmsg, gram_slot, gsend, gram_recv)

    drain(cmsg, cross_slot, csend, cross_recv)


def place_results(*refs):
    sources, targets, sems = refs[:3], refs[3:6], refs[6]
    copies = [
        pltpu.make_async_copy(source, target, sems.at[i])
        for i, (source, target) in enumerate(zip(sources, targets))
    ]
    for copy in copies:
        copy.start()
    for copy in copies:
        copy.wait()


def hosted_body(trial_block, response_weight):
    nl, rows, cols, depth = trial_block.shape
    groups, parts = lax.axis_size("grid"), lax.axis_size("vec")
    nvec, blocks = parts * nl, groups // 2
    length, wide_y, devices = blocks * rows, 2 * cols, groups * parts
    f32 = jnp.float32
    dma = pltpu.SemaphoreType.DMA
    vmem = pl.BlockSpec(memory_space=pltpu.VMEM)
    field = pltpu.VMEM((length, wide_y, depth), f32)
    padded = pltpu.VMEM((length, wide_y + 2 * PAD, depth), f32)
    whole = pltpu.VMEM((nvec, rows, cols, depth), f32)
    results = pl.pallas_call(
        functools.partial(kernel, groups, parts),
        out_shape=(
            pltpu.VMEM(trial_block.shape, f32),
            pltpu.VMEM(trial_block.shape, f32),
            pltpu.VMEM((nvec, nvec), f32),
        ),
        in_specs=[pl.BlockSpec(memory_space=pl.ANY)] * 2,
        out_specs=(vmem, vmem, vmem),
        scratch_shapes=[
            pltpu.VMEM((rows, cols, depth), f32),
            pltpu.VMEM((nl, rows, cols, depth), f32),
            padded, padded, padded, field, field, field,
            pltpu.VMEM((2 * depth, 2 * depth), jnp.bfloat16), whole, whole,
            pltpu.VMEM((2 * nl, depth), f32), pltpu.VMEM((2 * groups, 2 * nl, depth), f32),
            pltpu.VMEM((nl, depth), f32), pltpu.VMEM((devices, nl, depth), f32),
            pltpu.VMEM((3, nvec, depth), f32), pltpu.VMEM((nvec, nl, depth), f32),
            pltpu.SemaphoreType.REGULAR((1,)),
            dma((nl,)), dma((groups,)), dma((2,)), dma((3,)), dma((2,)), dma((2,)),
            dma((groups,)), dma((nl,)), dma((nl,)), dma((nl,)), dma((nl,)), dma((nl,)),
            dma((nl,)), dma((nl,)),
            dma((devices,)), dma((2 * groups,)), dma((devices,)), dma((devices,)), dma((2,)),
        ],
        compiler_params=pltpu.CompilerParams(collective_id=0, has_side_effects=True),
    )(trial_block, response_weight)
    return pl.pallas_call(
        place_results,
        out_shape=tuple(jax.ShapeDtypeStruct(part.shape, f32) for part in results),
        in_specs=[vmem] * 3,
        out_specs=(pl.BlockSpec(memory_space=pl.ANY),) * 3,
        scratch_shapes=[dma((3,))],
    )(*(pltpu.with_memory_space_constraint(part, pltpu.VMEM) for part in results))


def chosen_body(trial_block, response_weight):
    nl, rows, cols, depth = trial_block.shape
    groups, parts = lax.axis_size("grid"), lax.axis_size("vec")
    fits = (
        max(groups // 16, 2) == 2 and groups == 2 * nl and parts == nl
        and rows == HALO and cols % 8 == 0 and cols >= PAD and parts * nl <= depth
    )
    return (hosted_body if fits else body)(trial_block, response_weight)


def solution(mesh):
    placed = (P("vec", "grid", None, None), P("grid", None, None))
    return jax.shard_map(
        chosen_body,
        mesh=mesh,
        in_specs=placed,
        out_specs=(P("vec", "grid", None, None), P("vec", "grid", None, None), P()),
        check_vma=False,
    )
```
